256 devices in a mesh: expert: 64 (over z, y, core), tensor: 4 (over x).
Axes of the slice: x: 4, y: 4, z: 8, core: 2. Of those that a mesh axis runs over, the one named last changes fastest.
Arguments:
- tokens: bfloat16 [4096, 4096], P('expert', 'tensor'), may hold values from -6 to 6
- grad_out: bfloat16 [4096, 4096], P('expert', 'tensor'), may hold values from -6 to 6
- expert_ids: int32 [4096, 8], P('expert'), may hold values from 0 to 63, all different within a row; in each aligned block of 64 rows (0 to 63, 64 to 127, ...) at most 9 rows name the same one
- route_weights: bfloat16 [4096, 8], P('expert'), may hold values from 0.049804688 to 1
- gate_weights: bfloat16 [64, 4096, 1536], P('expert', None, 'tensor'), may hold values from -0.09375 to 0.09375
- up_weights: bfloat16 [64, 4096, 1536], P('expert', None, 'tensor'), may hold values from -0.09375 to 0.09375
- down_weights: bfloat16 [64, 1536, 4096], P('expert', 'tensor'), may hold values from -0.15625 to 0.15625
Outputs:
- grad_tokens: bfloat16 [4096, 4096], P('expert', 'tensor')
- grad_weights: bfloat16 [4096, 8], P('expert')
The draws below stay inside these ranges and needn't reach their ends.
Inputs may be any that keep to these rules, and one draw needn't show every extreme that they name: `expert_ids`: each row names 8 different experts. Among the 64 rows of one index of expert no expert is named by more than 9 rows, and in every draw some expert is named by exactly 9 rows of one index.
All inputs are finite; a program needn't handle non-finite values.
Results may differ from the reference program's by a relative error of at most 0.008.
Values may be sent and summed in bfloat16 or wider, within the bound.
A program may use at most 128 MiB of HBM per device.

```python
import math
import jax
import jax.numpy as jnp
import numpy as np
from jax import lax

D = 4096
FF = 1536
TOP = 8
TOK_DEV = 64
EXPERTS = 64
TOKENS = 4096
CAP = 9
N_EXPERT = 64
N_TENSOR = 4


def levels(stream_key, extent, cuts, smallest, top_value):
    loudness, own = 1.0, jax.random.fold_in(stream_key, 6)
    for dim, blocks in cuts:
        heights = jnp.exp(jax.random.uniform(jax.random.fold_in(own, dim), (blocks,), jnp.float32, smallest / len(cuts), top_value / len(cuts)))
        loudness = loudness * jnp.repeat(heights, extent[dim] // blocks).reshape([-1 if axis == dim else 1 for axis in range(len(extent))])
    return loudness


def routed_block(stream_key, own, number, rows, number_of, top, most, slope):
    order = jax.random.permutation(stream_key, number_of)
    heavy_load, ordinary = shares(number_of, rows * top, most, slope, True), shares(number_of, rows * top, most, slope, False)
    places = jnp.arange(number_of)

    def named(lengths, turn):
        used = int((lengths > 0).sum())
        fixed = max(1, used // 4)
        passed = fixed + (places - fixed + turn * (used - fixed)) % max(1, number_of - fixed)
        return jnp.zeros((number_of,), jnp.int32).at[order[jnp.where(places < fixed, places, passed)]].set(jnp.asarray(lengths, jnp.int32))

    lengths = jnp.where(number % 4 == 0, named(heavy_load, number // 4), named(ordinary, number - number // 4 - 1))
    mixed = jax.random.permutation(jax.random.fold_in(own, 3), number_of)
    donor, receiver = mixed[0:number_of // 2 * 2:2], mixed[1:number_of // 2 * 2:2]
    room = jnp.minimum(lengths[donor] - 1, most - lengths[receiver]) // 2
    room = jnp.where((donor == order[0]) | (receiver == order[0]) | (lengths[receiver] == 0), 0, jnp.maximum(room, 0))
    passed = jax.random.randint(jax.random.fold_in(own, 4), (number_of // 2,), 0, 1 << 20) % (room + 1)
    lengths = lengths.at[donor].add(-passed).at[receiver].add(passed)
    labels = jnp.searchsorted(jnp.cumsum(lengths), jnp.arange(rows * top), side="right").astype(jnp.int32)
    grid = labels.reshape(top, rows).T
    grid = grid[jax.random.permutation(jax.random.fold_in(own, 1), rows)]
    turn = jax.random.randint(jax.random.fold_in(own, 2), (rows, 1), 0, top)
    return jnp.take_along_axis(grid, (jnp.arange(top)[None, :] + turn) % top, axis=1)


def shares(number_of, total, limit, skew, full):
    loads = [(1 << 20) // math.isqrt(grade ** skew) + 1 for grade in range(1, number_of + 1)]
    largest = limit if full else min(limit, max(-(-total // number_of), total * loads[0] // sum(loads)))
    least = 1 if total - largest >= number_of - 1 else 0
    holding, rest = [largest] + [least] * (number_of - 1), total - largest - least * (number_of - 1)
    while rest > 0:
        free = [i for i in range(1, number_of) if holding[i] < largest] or [i for i in range(1, number_of) if holding[i] < limit]
        whole, left = sum([loads[i] for i in free]), rest
        for i in free:
            more = min(limit - holding[i], max(1, left * loads[i] // whole), rest)
            holding[i] = holding[i] + more
            rest = rest - more
    return np.array(holding)


def centred(key, extent, scale, reach, split=(), held_as=jnp.bfloat16):
    entries = jax.random.normal(key, extent, jnp.float32) * scale
    if len(split) > 0:
        entries = levels(key, extent, split, -0.22, 0.18) * entries
    return jnp.clip(entries, min=-reach, max=reach).astype(held_as)


def setup_inputs(seed: int = 0) -> dict:
    key_of = jax.random.split(jax.random.key(seed), 8)
    tokens = centred(key_of[0], (TOKENS, D), 1.0, 6.0, ((0, 64), (1, 4)))
    grad_out = centred(key_of[1], (TOKENS, D), 1.0, 6.0, ((0, 64), (1, 4)))
    expert_ids_keys = jax.random.split(jax.random.fold_in(key_of[2], 1), TOKENS // TOK_DEV)
    expert_ids_turns = jax.random.permutation(jax.random.fold_in(key_of[2], 3), TOKENS // TOK_DEV)
    expert_ids = jax.vmap(lambda own, number: routed_block(jax.random.fold_in(key_of[2], 2), own, number, TOK_DEV, EXPERTS, TOP, CAP, 2))(expert_ids_keys, expert_ids_turns).reshape((TOKENS, TOP))
    route_weights = jnp.clip(0.049804688 + 0.9501953 * jax.random.uniform(key_of[3], (TOKENS, TOP), jnp.float32) ** levels(key_of[3], (TOKENS, TOP), ((0, 64),), -0.2, 0.2), 0.049804688, 1.0).astype(jnp.bfloat16)
    gate_weights = centred(key_of[4], (EXPERTS, D, FF), D ** -0.5, 0.09375, ((0, 64), (2, 4)))
    up_weights = centred(key_of[5], (EXPERTS, D, FF), D ** -0.5, 0.09375, ((0, 64), (2, 4)))
    down_weights = centred(key_of[6], (EXPERTS, FF, D), FF ** -0.5, 0.15625, ((0, 64), (1, 4)))
    return {"tokens": tokens, "grad_out": grad_out, "expert_ids": expert_ids, "route_weights": route_weights, "gate_weights": gate_weights, "up_weights": up_weights, "down_weights": down_weights}


def route_slots(flat_ids, experts, capacity):
    onehot = (flat_ids[:, None] == jnp.arange(experts, dtype=jnp.int32)[None, :]).astype(jnp.int32)
    before = jnp.cumsum(onehot, axis=0) - onehot
    position = jnp.sum(before * onehot, axis=1)
    target = flat_ids * capacity + position
    routes = flat_ids.shape[0]
    return jnp.full((experts * capacity,), -1, jnp.int32).at[target].set(jnp.arange(routes, dtype=jnp.int32))


def expert_block(inputs, grads, scales, gate_weight, up_weight, down_weight):
    contract = (((1,), (1,)), ((), ()))
    gate_vals = jnp.dot(inputs, gate_weight, preferred_element_type=jnp.float32)
    up_vals = jnp.dot(inputs, up_weight, preferred_element_type=jnp.float32)
    back_vals = lax.dot_general(grads, down_weight, contract, preferred_element_type=jnp.float32)
    sigmoid = jax.nn.sigmoid(gate_vals)
    active = gate_vals * sigmoid
    weight_grad = jnp.sum(active * up_vals * back_vals, axis=1)
    scaled = scales[:, None] * back_vals
    gate_grad = (scaled * up_vals * sigmoid * (1.0 + gate_vals * (1.0 - sigmoid))).astype(jnp.bfloat16)
    up_grad = (scaled * active).astype(jnp.bfloat16)
    input_grad = lax.dot_general(gate_grad, gate_weight, contract, preferred_element_type=jnp.float32)
    input_grad = input_grad + lax.dot_general(up_grad, up_weight, contract, preferred_element_type=jnp.float32)
    return input_grad.astype(jnp.bfloat16), weight_grad


def reference(tokens, grad_out, expert_ids, route_weights, gate_weights, up_weights, down_weights):
    per_block = expert_ids.reshape(N_EXPERT, TOK_DEV * TOP)
    local_slots = jax.vmap(lambda flat_ids: route_slots(flat_ids, EXPERTS, CAP))(per_block)
    offsets = (jnp.arange(N_EXPERT, dtype=jnp.int32) * (TOK_DEV * TOP))[:, None]
    global_slots = jnp.where(local_slots >= 0, local_slots + offsets, -1)
    slots_by_expert = jnp.transpose(global_slots.reshape(N_EXPERT, EXPERTS, CAP), (1, 0, 2)).reshape(EXPERTS, N_EXPERT * CAP)
    flat_weights = route_weights.reshape(-1)
    quarter = FF // N_TENSOR

    def per_expert(carry, pieces):
        grad_acc, weight_acc = carry
        gate_weight, up_weight, down_weight, slot_route = pieces
        live_mask = slot_route >= 0
        safe_route = jnp.where(live_mask, slot_route, 0)
        owner_rows = safe_route // TOP
        inputs = jnp.where(live_mask[:, None], tokens[owner_rows], jnp.zeros((), jnp.bfloat16))
        grads = jnp.where(live_mask[:, None], grad_out[owner_rows], jnp.zeros((), jnp.bfloat16))
        scales = jnp.where(live_mask, flat_weights[safe_route].astype(jnp.float32), jnp.zeros((), jnp.float32))
        total = jnp.zeros((inputs.shape[0], D), jnp.float32)
        weight_total = jnp.zeros((inputs.shape[0],), jnp.float32)
        for group in range(N_TENSOR):
            lower = group * quarter
            part, weight_part = expert_block(inputs, grads, scales, gate_weight[:, lower:lower + quarter], up_weight[:, lower:lower + quarter], down_weight[lower:lower + quarter, :])
            total = total + part.astype(jnp.float32)
            weight_total = weight_total + weight_part
        grad_acc = grad_acc.at[owner_rows].add(jnp.where(live_mask[:, None], total, jnp.zeros((), jnp.float32)))
        weight_acc = weight_acc.at[safe_route].add(jnp.where(live_mask, weight_total, jnp.zeros((), jnp.float32)))
        return (grad_acc, weight_acc), None

    start = (jnp.zeros((TOKENS, D), jnp.float32), jnp.zeros((TOKENS * TOP,), jnp.float32))
    (grad_acc, weight_acc), unused = lax.scan(per_expert, start, (gate_weights, up_weights, down_weights, slots_by_expert))
    return grad_acc.astype(jnp.bfloat16), weight_acc.reshape(TOKENS, TOP).astype(jnp.bfloat16)
```

```python
import jax
import jax.numpy as jnp
from jax import lax
from jax.sharding import PartitionSpec as P

TOP = 8


def expert_rows(inputs, grads, scales, gate_weight, up_weight, down_weight):
    contract = (((1,), (1,)), ((), ()))
    gate_vals = jnp.dot(inputs, gate_weight, preferred_element_type=jnp.float32)
    up_vals = jnp.dot(inputs, up_weight, preferred_element_type=jnp.float32)
    back_vals = lax.dot_general(grads, down_weight, contract, preferred_element_type=jnp.float32)
    sigmoid = jax.nn.sigmoid(gate_vals)
    active = gate_vals * sigmoid
    weight_grad = jnp.sum(active * up_vals * back_vals, axis=1)
    scaled = scales * back_vals
    gate_grad = (scaled * up_vals * sigmoid * (1.0 + gate_vals * (1.0 - sigmoid))).astype(
        jnp.bfloat16
    )
    up_grad = (scaled * active).astype(jnp.bfloat16)
    input_grad = lax.dot_general(
        gate_grad, gate_weight, contract, preferred_element_type=jnp.float32
    )
    input_grad = input_grad + lax.dot_general(
        up_grad, up_weight, contract, preferred_element_type=jnp.float32
    )
    return input_grad.astype(jnp.bfloat16), weight_grad


def body(tokens, grad_out, expert_ids, route_weights, gate_weights, up_weights, down_weights):
    experts = lax.axis_size("expert")
    rows, width = tokens.shape
    capacity = min(rows, max(2, 7 * rows * TOP // (6 * experts)))
    hit = expert_ids[:, :, None] == jnp.arange(experts, dtype=jnp.int32)
    named = jnp.any(hit, axis=1)
    below = jnp.tril(jnp.ones((rows, rows), jnp.bfloat16), -1)
    place = jnp.dot(below, named.astype(jnp.bfloat16), preferred_element_type=jnp.float32)
    scale = jnp.sum(jnp.where(hit, route_weights[:, :, None].astype(jnp.float32), 0.0), axis=1)
    slot = jnp.arange(capacity, dtype=jnp.float32)
    select = named[:, :, None] & (place[:, :, None] == slot)
    picked = select.astype(jnp.bfloat16)
    spread = picked.reshape(rows, experts * capacity)
    slot_scale = jnp.sum(jnp.where(select, scale[:, :, None], 0.0), axis=0)
    both = jnp.concatenate([tokens, grad_out], axis=1)
    sent = lax.dot_general(
        spread, both, (((0,), (0,)), ((), ())), preferred_element_type=jnp.float32
    ).astype(jnp.bfloat16)
    tail = jnp.broadcast_to(slot_scale.reshape(-1, 1), (experts * capacity, 128))
    sent = jnp.concatenate([sent, tail.astype(jnp.bfloat16)], axis=1)
    got = lax.all_to_all(sent, "expert", split_axis=0, concat_axis=0, tiled=True)
    got_tokens = lax.all_gather(got[:, :width], "tensor", axis=1, tiled=True)
    got_grads = lax.all_gather(got[:, width : 2 * width], "tensor", axis=1, tiled=True)
    scales = got[:, 2 * width : 2 * width + 1].astype(jnp.float32)
    grad_rows, weight_rows = expert_rows(
        got_tokens, got_grads, scales, gate_weights[0], up_weights[0], down_weights[0]
    )
    weight_total = lax.psum(weight_rows, "tensor").astype(jnp.bfloat16)
    summed = lax.psum_scatter(grad_rows, "tensor", scatter_dimension=1, tiled=True)
    tail = jnp.broadcast_to(weight_total[:, None], (experts * capacity, 128))
    back = lax.all_to_all(
        jnp.concatenate([summed, tail], axis=1), "expert", split_axis=0, concat_axis=0, tiled=True
    )
    input_grads = jnp.dot(
        spread, back[:, :width], preferred_element_type=jnp.float32
    ).astype(jnp.bfloat16)
    route = back[:, width].astype(jnp.float32).reshape(experts, capacity)
    per_pair = jnp.sum(jnp.where(select, route, 0.0), axis=2)
    route_grads = jnp.sum(jnp.where(hit, per_pair[:, None, :], 0.0), axis=2)
    return input_grads, route_grads.astype(jnp.bfloat16)


def solution(mesh):
    in_specs = (
        P("expert", "tensor"),
        P("expert", "tensor"),
        P("expert", None),
        P("expert", None),
        P("expert", None, "tensor"),
        P("expert", None, "tensor"),
        P("expert", "tensor", None),
    )
    out_specs = (P("expert", "tensor"), P("expert", None))
    return jax.shard_map(body, mesh=mesh, in_specs=in_specs, out_specs=out_specs, check_vma=False)
```

```python
import jax
import jax.numpy as jnp
from jax import lax
from jax.experimental import pallas as pl
from jax.experimental.pallas import tpu as pltpu
from jax.sharding import PartitionSpec as P

NZ, NY, NC, NX = 8, 4, 2, 4
TOP = 8
CAP = 9
ROWS = 64
SLOTS = NZ * NC
CH = SLOTS * CAP
W = 1024
HALF = W // 2
FH = 384
META = 128
ORDER = (0, 1, 3, 2)
MESH = pl.DeviceIdType.MESH
F32 = jnp.float32
BF = jnp.bfloat16
NT = (((1,), (1,)), ((), ()))


def dot(a, b):
    return jnp.dot(a, b, preferred_element_type=F32)


def dot_nt(a, b):
    return lax.dot_general(a, b, NT, preferred_element_type=F32)


def iota(shape, dim):
    return lax.broadcasted_iota(jnp.int32, shape, dim)


def kernel(
    tok_ref, grd_ref, ids_ref, rw_ref, wg_ref, wu_ref, wd_ref,
    gt_ref, gw_ref,
    xt, xg, pick, put, st, sg, rt, rg, rtx, rgx, wgu, wdv, gu, dd, ha, hb, fl, fr,
    vv, qq, yy, tw, bb, ff, gx, gv, gq, gl, ga, code_ref,
    w_sem, zrt, zrg, zst, zsg, yrt, yrg, yst, ysg, xrt, xrg, xst, xsg,
    cxr, cxs, gxr, gxs, cyr, cys, gyr, gys, twr, tws, zcr, zcs, gzr, gzs,
):
    me = lax.axis_index("expert")
    x = lax.axis_index("tensor")
    z = me // (NY * NC)
    y = (me // NC) % NY
    c = me % NC

    def dev(dz=0, dy=0, dc=0, dx=0):
        e = (((z + dz) % NZ) * NY + (y + dy) % NY) * NC + (c + dc) % NC
        return (e, (x + dx) % NX)

    def remote(src, dst, ssem, rsem, where):
        return pltpu.make_async_remote_copy(
            src_ref=src, dst_ref=dst, send_sem=ssem, recv_sem=rsem,
            device_id=where, device_id_type=MESH,
        )

    sends = []

    def send(*args):
        copy = remote(*args)
        copy.start()
        sends.append(copy)

    def arrived(dst, rsem):
        remote(dst, dst, rsem, rsem, dev(dz=1)).wait_recv()

    loads = []
    for r in range(NX):
        at = pl.multiple_of(((x + r) % NX) * W, W)
        loads.append(pltpu.make_async_copy(
            wg_ref.at[0, pl.ds(at, W), :], wgu.at[r, :, 0:FH], w_sem.at[3 * r]))
        loads.append(pltpu.make_async_copy(
            wu_ref.at[0, pl.ds(at, W), :], wgu.at[r, :, FH:2 * FH], w_sem.at[3 * r + 1]))
        loads.append(pltpu.make_async_copy(
            wd_ref.at[0, :, pl.ds(at, W)], wdv.at[r], w_sem.at[3 * r + 2]))
    for load in loads:
        load.start()

    barrier = pltpu.get_barrier_semaphore()
    partners = [dev(dz=d, dc=k) for d in range(NZ) for k in range(NC) if d or k]
    partners += [dev(dy=d) for d in range(1, NY)] + [dev(dx=d) for d in range(1, NX)]
    for partner in partners:
        pl.semaphore_signal(barrier, inc=1, device_id=partner, device_id_type=MESH)

    lane = iota((ROWS, META), 1)
    named = jnp.zeros((ROWS, META), F32)
    weight = jnp.zeros((ROWS, META), F32)
    for k in range(TOP):
        idk = ids_ref[:, k:k + 1]
        named = named + jnp.where(lane == idk, 1.0, 0.0)
        weight = weight + jnp.where(lane == idk + 64, rw_ref[:, k:k + 1], 0.0)
    below = (iota((ROWS, ROWS), 0) > iota((ROWS, ROWS), 1)).astype(F32).astype(BF)
    code = named * (dot(below, named.astype(BF)) + 1.0)
    code_ref[...] = code
    xt[0, :, 0:W] = tok_ref[...]
    xt[0, :, W:W + META] = (code + weight).astype(BF)
    xg[0] = grd_ref[...]
    gx[...] = jnp.zeros_like(gx)

    pl.semaphore_wait(barrier, len(partners))

    def ring(buf, slot, rsem, ssem):
        if slot == 0:
            send(buf.at[0], buf.at[7], ssem.at[0], rsem.at[7], dev(dz=1))
            send(buf.at[0], buf.at[1], ssem.at[8], rsem.at[1], dev(dz=NZ - 1))
        elif slot > 4:
            send(buf.at[slot], buf.at[slot - 1], ssem.at[slot], rsem.at[slot - 1], dev(dz=1))
        elif slot < 3:
            send(
                buf.at[slot], buf.at[slot + 1], ssem.at[slot], rsem.at[slot + 1], dev(dz=NZ - 1)
            )
        send(buf.at[slot], buf.at[slot + 8], ssem.at[slot + 9], rsem.at[slot + 8], dev(dc=1))

    def step(buf, s, rsem, ssem):
        for slot in ((8 - s, s) if s < 4 else (4,)):
            arrived(buf.at[slot], rsem.at[slot])
            ring(buf, slot, rsem, ssem)

    tok_z = (zrt, zst)
    grd_z = (zrg, zsg)
    ring(xt, 0, *tok_z)
    step(xt, 1, *tok_z)
    ring(xg, 0, *grd_z)
    step(xt, 2, *tok_z)
    step(xg, 1, *grd_z)
    step(xt, 3, *tok_z)
    step(xg, 2, *grd_z)
    step(xt, 4, *tok_z)
    for slot in range(8, 16):
        arrived(xt.at[slot], zrt.at[slot])

    tokens = SLOTS * ROWS
    meta = xt[:, :, W:W + META].reshape(tokens, META)
    for g in range(NY):
        e = (z * NY + (y + g) % NY) * NC + c
        choose = (iota((CH, META), 1) == e).astype(F32).astype(BF)
        got = dot_nt(choose, meta)
        row, col = iota((CH, tokens), 0), iota((CH, tokens), 1)
        hit = (got == (row % CAP + 1).astype(F32)) & (row // CAP == col // ROWS)
        pick[g * CH:(g + 1) * CH, :] = jnp.where(hit, 1.0, 0.0).astype(BF)

    def gather(buf, width, own, out, rows):
        data = buf[...].reshape(tokens, width)
        own[0] = dot(pick[0:CH, :], data).astype(BF)
        rows()
        rest = dot(pick[CH:NY * CH, :], data).astype(BF)
        out[...] = rest.reshape(NY - 1, CH, width)

    def x_first(o, own, ext, ssem, rsem):
        send(own.at[o, :, 0:W], ext.at[2, o], ssem.at[o, 0], rsem.at[o, 0], dev(dx=1))
        send(own.at[o, :, 0:W], ext.at[0, o], ssem.at[o, 1], rsem.at[o, 1], dev(dx=NX - 1))

    def x_second(o, ext, ssem, rsem):
        arrived(ext.at[2, o], rsem.at[o, 0])
        send(ext.at[2, o, :, 0:HALF], ext.at[1, o, :, 0:HALF], ssem.at[o, 2], rsem.at[o, 2], dev(dx=1))
        arrived(ext.at[0, o], rsem.at[o, 1])
        send(
            ext.at[0, o, :, HALF:W], ext.at[1, o, :, HALF:W],
            ssem.at[o, 3], rsem.at[o, 3], dev(dx=NX - 1),
        )

    def x_third(o, ext, rsem):
        arrived(ext.at[1, o, :, 0:HALF], rsem.at[o, 2])
        arrived(ext.at[1, o, :, HALF:W], rsem.at[o, 3])

    def y_send(out, own, ssem, rsem):
        for g in (3, 1, 2):
            o = (NY - g) % NY
            send(out.at[g - 1], own.at[o], ssem.at[g], rsem.at[o], dev(dy=g))

    tok_x = (xst, xrt)
    grd_x = (xsg, xrg)
    step(xg, 3, *grd_z)
    gather(xt, W + META, rt, st, lambda: x_first(0, rt, rtx, *tok_x))
    y_send(st, rt, yst, yrt)
    step(xg, 4, *grd_z)
    for slot in range(8, 16):
        arrived(xg.at[slot], zrg.at[slot])
    gather(xg, W, rg, sg, lambda: None)
    y_send(sg, rg, ysg, yrg)
    for load in loads:
        load.wait()
    for j in range(1, NY):
        arrived(rt.at[ORDER[j]], yrt.at[ORDER[j]])
        x_first(ORDER[j], rt, rtx, *tok_x)
        x_second(ORDER[j - 1], rtx, *tok_x)
    x_first(0, rg, rgx, *grd_x)
    x_second(ORDER[3], rtx, *tok_x)

    def quarter(own, ext, o, r):
        return own[o, :, 0:W] if r == 0 else ext[r - 1, o]

    def forward(o):
        x_third(o, rtx, xrt)
        total = dot(quarter(rt, rtx, o, 0), wgu[0])
        for r in range(1, NX):
            total = total + dot(quarter(rt, rtx, o, r), wgu[r])
        gu[o] = total

    for j in range(NY):
        if j:
            arrived(rg.at[ORDER[j]], yrg.at[ORDER[j]])
            x_first(ORDER[j], rg, rgx, *grd_x)
            x_second(ORDER[j - 1], rgx, *grd_x)
        forward(ORDER[j])
    x_second(ORDER[3], rgx, *grd_x)

    ones = jnp.ones((8, FH), BF)

    def backward(o):
        x_third(o, rgx, xrg)
        back = dot_nt(quarter(rg, rgx, o, 0), wdv[0])
        for r in range(1, NX):
            back = back + dot_nt(quarter(rg, rgx, o, r), wdv[r])
        gate = gu[o, :, 0:FH]
        up = gu[o, :, FH:2 * FH]
        sig = 1.0 / (1.0 + jnp.exp(-gate))
        act = gate * sig
        prod = act * up * back
        high = prod.astype(BF)
        low = (prod - high.astype(F32)).astype(BF)
        gx[0, o, :, 0:CH] = dot_nt(ones, high) + dot_nt(ones, low)
        for k, d in enumerate((1, 3, 2)):
            send(gx.at[0, o], gx.at[NX - d, o], gxs.at[o, k], gxr.at[o, k], dev(dx=d))
        rows = rt[o, :, W:W + META].astype(F32)
        scale = jnp.sum(
            jnp.where(iota((CH, META), 1) == me + 64, rows, 0.0), axis=1, keepdims=True
        )
        scaled = scale * back
        dgate = (scaled * up * sig * (1.0 + gate * (1.0 - sig))).astype(BF)
        dup = (scaled * act).astype(BF)
        both = jnp.concatenate([dgate, dup], axis=1)
        dd[2, o] = dot_nt(both, wgu[2]).astype(BF)
        send(dd.at[2, o, :, 0:HALF], ha.at[o], cxs.at[o, 0], cxr.at[o, 0], dev(dx=1))
        send(dd.at[2, o, :, HALF:W], hb.at[o], cxs.at[o, 1], cxr.at[o, 1], dev(dx=NX - 1))
        for r in (1, 3, 0):
            dd[r, o] = dot_nt(both, wgu[r]).astype(BF)

    def sum_second(o):
        arrived(ha.at[o], cxr.at[o, 0])
        dd[1, o, :, 0:HALF] = (dd[1, o, :, 0:HALF].astype(F32) + ha[o].astype(F32)).astype(BF)
        send(dd.at[1, o], fl.at[o], cxs.at[o, 2], cxr.at[o, 2], dev(dx=1))
        arrived(hb.at[o], cxr.at[o, 1])
        dd[3, o, :, HALF:W] = (dd[3, o, :, HALF:W].astype(F32) + hb[o].astype(F32)).astype(BF)
        send(dd.at[3, o], fr.at[o], cxs.at[o, 3], cxr.at[o, 3], dev(dx=NX - 1))

    def sum_third(o):
        g = (NY - o) % NY
        for k, d in enumerate((1, 3, 2)):
            arrived(gx.at[NX - d, o], gxr.at[o, k])
        parts = (gx[0, o] + gx[1, o]) + (gx[2, o] + gx[3, o])
        arrived(fl.at[o], cxr.at[o, 2])
        arrived(fr.at[o], cxr.at[o, 3])
        total = dd[0, o].astype(F32) + fl[o].astype(F32) + fr[o].astype(F32)
        if o == 0:
            qq[0] = total.astype(BF)
            gq[0] = parts
        else:
            vv[o] = total.astype(BF)
            gv[o] = parts
            send(vv.at[o], qq.at[g], cys.at[o], cyr.at[g], dev(dy=o))
            send(gv.at[o], gq.at[g], gys.at[o], gyr.at[g], dev(dy=o))

    for j in range(NY):
        backward(ORDER[j])
        if j:
            sum_second(ORDER[j - 1])
        if j > 1:
            sum_third(ORDER[j - 2])
    sum_second(ORDER[3])
    sum_third(ORDER[2])

    for g in range(NY):
        e = (z * NY + (y + g) % NY) * NC + c
        choose = (iota((META, CH), 0) == e).astype(F32).astype(BF)
        got = dot(meta, choose)
        row, col = iota((tokens, CH), 1), iota((tokens, CH), 0)
        hit = (got == (row % CAP + 1).astype(F32)) & (row // CAP == col // ROWS)
        put[g] = jnp.where(hit, 1.0, 0.0).astype(BF)

    sum_third(ORDER[3])
    for g in range(1, NY):
        arrived(gq.at[g], gyr.at[g])
    rows8 = iota((8, 2 * META), 0)
    mine = jnp.zeros((8, 2 * META), F32)
    for g in range(NY):
        mine = mine + jnp.where(rows8 == g, gq[g], 0.0)
    gl[...] = mine
    ga[0] = mine
    for g in range(1, NY):
        arrived(qq.at[g], cyr.at[g])
    half = tokens // 2

    def spread(lo):
        total = dot(put[0, lo:lo + half, :], qq[0])
        for g in range(1, NY):
            total = total + dot(put[g, lo:lo + half, :], qq[g])
        return total

    yy[...] = spread(half).astype(BF).reshape(NZ, ROWS, W)
    send(yy, tw, tws.at[0], twr.at[0], dev(dc=1))
    for k in range(NC):
        for d in range(NZ):
            if d or k:
                slot = k * 8 + d
                back_slot = k * 8 + (NZ - d) % NZ
                send(gl, ga.at[back_slot], gzs.at[slot], gzr.at[back_slot], dev(dz=d, dc=k))
    own = spread(0)
    arrived(tw, twr.at[0])
    own = own.reshape(NZ, ROWS, W) + tw[...].astype(F32)
    bb[...] = own.astype(BF)
    for d in (4, 3, 5, 2, 6, 1, 7):
        send(bb.at[d], ff.at[(NZ - d) % NZ], zcs.at[d], zcr.at[(NZ - d) % NZ], dev(dz=d))

    for slot in range(1, SLOTS):
        arrived(ga.at[slot], gzr.at[slot])
    table = ga[...].reshape(SLOTS * 8, 2 * META)
    high = table.astype(BF)
    low = (table - high.astype(F32)).astype(BF)
    code = code_ref[...]
    lane8 = iota((ROWS, TOP), 1)
    result = jnp.zeros((ROWS, TOP), F32)
    for k in range(TOP):
        idk = ids_ref[:, k:k + 1]
        place = jnp.sum(jnp.where(lane == idk, code, 0.0), axis=1, keepdims=True)
        dz = ((idk >> 3) - z) & 7
        dy = ((idk >> 1) - y) & 3
        dc = (idk - c) & 1
        wanted = (dc * 8 + dz) * 8 + dy
        line = (dc * 8 + ((8 - dz) & 7)) * CAP
        onehot = (lane == wanted).astype(F32).astype(BF)
        values = dot(onehot, high) + dot(onehot, low)
        at = iota((ROWS, 2 * META), 1) - line + 1
        value = jnp.sum(jnp.where(at.astype(F32) == place, values, 0.0), axis=1, keepdims=True)
        result = result + jnp.where(lane8 == k, value, 0.0)
    gw_ref[...] = result.astype(BF)

    total = bb[0].astype(F32)
    for d in range(1, NZ):
        arrived(ff.at[d], zcr.at[d])
        total = total + ff[d].astype(F32)
    gt_ref[...] = total.astype(BF)
    for copy in sends:
        copy.wait_send()


def body(tokens, grad_out, expert_ids, route_weights, gate_weights, up_weights, down_weights):
    vmem = pl.BlockSpec(memory_space=pltpu.VMEM)
    hbm = pl.BlockSpec(memory_space=pl.ANY)
    V = pltpu.VMEM
    D = pltpu.SemaphoreType.DMA
    n_tok = SLOTS * ROWS
    scratch = [
        V((SLOTS, ROWS, W + META), BF), V((SLOTS, ROWS, W), BF),
        V((NY * CH, n_tok), BF), V((NY, n_tok, CH), BF),
        V((NY - 1, CH, W + META), BF), V((NY - 1, CH, W), BF),
        V((NY, CH, W + META), BF), V((NY, CH, W), BF),
        V((NX - 1, NY, CH, W), BF), V((NX - 1, NY, CH, W), BF),
        V((NX, W, 2 * FH), BF), V((NX, FH, W), BF),
        V((NY, CH, 2 * FH), F32), V((NX, NY, CH, W), BF),
        V((NY, CH, HALF), BF), V((NY, CH, HALF), BF), V((NY, CH, W), BF), V((NY, CH, W), BF),
        V((NY, CH, W), BF), V((NY, CH, W), BF),
        V((NZ, ROWS, W), BF), V((NZ, ROWS, W), BF), V((NZ, ROWS, W), BF), V((NZ, ROWS, W), BF),
        V((NX, NY, 8, 2 * META), F32), V((NY, 8, 2 * META), F32), V((NY, 8, 2 * META), F32),
        V((8, 2 * META), F32), V((SLOTS, 8, 2 * META), F32), V((ROWS, META), F32),
        D((12,)),
        D((16,)), D((16,)), D((17,)), D((17,)),
        D((4,)), D((4,)), D((4,)), D((4,)),
        D((4, 4)), D((4, 4)), D((4, 4)), D((4, 4)),
        D((4, 4)), D((4, 4)), D((4, 3)), D((4, 3)),
        D((4,)), D((4,)), D((4,)), D((4,)),
        D((1,)), D((1,)), D((8,)), D((8,)), D((16,)), D((16,)),
    ]
    return pl.pallas_call(
        kernel,
        out_shape=(
            jax.ShapeDtypeStruct(tokens.shape, BF),
            jax.ShapeDtypeStruct(expert_ids.shape, BF),
        ),
        in_specs=[vmem, vmem, vmem, vmem, hbm, hbm, hbm],
        out_specs=(vmem, vmem),
        scratch_shapes=scratch,
        compiler_params=pltpu.CompilerParams(
            collective_id=0, has_side_effects=True, vmem_limit_bytes=66 * 1000 * 1000
        ),
    )(
        tokens, grad_out, expert_ids, route_weights.astype(F32),
        gate_weights, up_weights, down_weights,
    )


def solution(mesh):
    in_specs = (
        P("expert", "tensor"),
        P("expert", "tensor"),
        P("expert", None),
        P("expert", None),
        P("expert", None, "tensor"),
        P("expert", None, "tensor"),
        P("expert", "tensor", None),
    )
    out_specs = (P("expert", "tensor"), P("expert", None))
    return jax.shard_map(body, mesh=mesh, in_specs=in_specs, out_specs=out_specs, check_vma=False)
```

```python
import jax
import jax.numpy as jnp
from jax import lax
from jax.experimental import pallas as pl
from jax.experimental.pallas import tpu as pltpu
from jax.sharding import PartitionSpec as P

NZ, NY, NC, NX = 8, 4, 2, 4
TOP = 8
CAP = 9
ROWS = 64
SLOTS = NZ * NC
CH = SLOTS * CAP
W = 1024
HALF = W // 2
FH = 384
META = 128
ORDER = (0, 1, 3, 2)
BACK = (1, 2, 3, 0)
MESH = pl.DeviceIdType.MESH
F32 = jnp.float32
BF = jnp.bfloat16
NT = (((1,), (1,)), ((), ()))


def dot(a, b):
    return jnp.dot(a, b, preferred_element_type=F32)


def dot_nt(a, b):
    return lax.dot_general(a, b, NT, preferred_element_type=F32)


def iota(shape, dim):
    return lax.broadcasted_iota(jnp.int32, shape, dim)


def kernel(
    tok_ref, grd_ref, ids_ref, rw_ref, wg_ref, wu_ref, wd_ref,
    gt_ref, gw_ref,
    xt, xg, pick, put, st, sg, rt, rg, rtx, rgx, wgu, wdv, gu, dd, ha, hb, fl, fr,
    vv, qq, yy, tw, bb, ff, gx, gv, gq, gl, ga, code_ref, acc,
    w_sem, zrt, zrg, zst, zsg, yrt, yrg, yst, ysg, xrt, xrg, xst, xsg,
    cxr, cxs, gxr, gxs, cyr, cys, gyr, gys, twr, tws, zcr, zcs, gzr, gzs,
):
    me = lax.axis_index("expert")
    x = lax.axis_index("tensor")
    z = me // (NY * NC)
    y = (me // NC) % NY
    c = me % NC

    def dev(dz=0, dy=0, dc=0, dx=0):
        e = (((z + dz) % NZ) * NY + (y + dy) % NY) * NC + (c + dc) % NC
        return (e, (x + dx) % NX)

    def remote(src, dst, ssem, rsem, where):
        return pltpu.make_async_remote_copy(
            src_ref=src, dst_ref=dst, send_sem=ssem, recv_sem=rsem,
            device_id=where, device_id_type=MESH,
        )

    sends = []

    def send(*args):
        copy = remote(*args)
        copy.start()
        sends.append(copy)

    def arrived(dst, rsem):
        remote(dst, dst, rsem, rsem, dev(dz=1)).wait_recv()

    loads = []
    for r in range(NX):
        at = pl.multiple_of(((x + r) % NX) * W, W)
        loads.append(pltpu.make_async_copy(
            wg_ref.at[0, pl.ds(at, W), :], wgu.at[r, :, 0:FH], w_sem.at[3 * r]))
        loads.append(pltpu.make_async_copy(
            wu_ref.at[0, pl.ds(at, W), :], wgu.at[r, :, FH:2 * FH], w_sem.at[3 * r + 1]))
        loads.append(pltpu.make_async_copy(
            wd_ref.at[0, :, pl.ds(at, W)], wdv.at[r], w_sem.at[3 * r + 2]))
    for load in loads:
        load.start()

    barrier = pltpu.get_barrier_semaphore()
    partners = [dev(dz=d, dc=k) for d in range(NZ) for k in range(NC) if d or k]
    partners += [dev(dy=d) for d in range(1, NY)] + [dev(dx=d) for d in range(1, NX)]
    for partner in partners:
        pl.semaphore_signal(barrier, inc=1, device_id=partner, device_id_type=MESH)

    lane = iota((ROWS, META), 1)
    named = jnp.zeros((ROWS, META), F32)
    weight = jnp.zeros((ROWS, META), F32)
    for k in range(TOP):
        idk = ids_ref[:, k:k + 1]
        named = named + jnp.where(lane == idk, 1.0, 0.0)
        weight = weight + jnp.where(lane == idk + 64, rw_ref[:, k:k + 1], 0.0)
    below = (iota((ROWS, ROWS), 0) > iota((ROWS, ROWS), 1)).astype(F32).astype(BF)
    code = named * (dot(below, named.astype(BF)) + 1.0)
    code_ref[...] = code
    xt[0, :, 0:W] = tok_ref[...]
    xt[0, :, W:W + META] = (code + weight).astype(BF)
    xg[0] = grd_ref[...]
    gx[...] = jnp.zeros_like(gx)

    pl.semaphore_wait(barrier, len(partners))

    def ring(buf, slot, rsem, ssem):
        if slot == 0:
            send(buf.at[0], buf.at[7], ssem.at[0], rsem.at[7], dev(dz=1))
            send(buf.at[0], buf.at[1], ssem.at[8], rsem.at[1], dev(dz=NZ - 1))
        elif slot > 4:
            send(buf.at[slot], buf.at[slot - 1], ssem.at[slot], rsem.at[slot - 1], dev(dz=1))
        elif slot < 3:
            send(
                buf.at[slot], buf.at[slot + 1], ssem.at[slot], rsem.at[slot + 1], dev(dz=NZ - 1)
            )
        send(buf.at[slot], buf.at[slot + 8], ssem.at[slot + 9], rsem.at[slot + 8], dev(dc=1))

    def step(buf, s, rsem, ssem):
        for slot in ((8 - s, s) if s < 4 else (4,)):
            arrived(buf.at[slot], rsem.at[slot])
            ring(buf, slot, rsem, ssem)

    tok_z = (zrt, zst)
    grd_z = (zrg, zsg)
    ring(xt, 0, *tok_z)
    step(xt, 1, *tok_z)
    ring(xg, 0, *grd_z)
    step(xt, 2, *tok_z)
    step(xg, 1, *grd_z)
    step(xt, 3, *tok_z)
    step(xg, 2, *grd_z)
    step(xt, 4, *tok_z)
    for slot in range(8, 16):
        arrived(xt.at[slot], zrt.at[slot])

    tokens = SLOTS * ROWS
    meta = xt[:, :, W:W + META].reshape(tokens, META)
    for g in range(NY):
        e = (z * NY + (y + g) % NY) * NC + c
        choose = (iota((CH, META), 1) == e).astype(F32).astype(BF)
        got = dot_nt(choose, meta)
        row, col = iota((CH, tokens), 0), iota((CH, tokens), 1)
        hit = (got == (row % CAP + 1).astype(F32)) & (row // CAP == col // ROWS)
        pick[g * CH:(g + 1) * CH, :] = jnp.where(hit, 1.0, 0.0).astype(BF)

    def gather(buf, width, own, out, rows):
        data = buf[...].reshape(tokens, width)
        own[0] = dot(pick[0:CH, :], data).astype(BF)
        rows()
        rest = dot(pick[CH:NY * CH, :], data).astype(BF)
        out[...] = rest.reshape(NY - 1, CH, width)

    def x_first(o, own, ext, ssem, rsem):
        send(own.at[o, :, 0:W], ext.at[2, o], ssem.at[o, 0], rsem.at[o, 0], dev(dx=1))
        send(own.at[o, :, 0:W], ext.at[0, o], ssem.at[o, 1], rsem.at[o, 1], dev(dx=NX - 1))

    def x_second(o, ext, ssem, rsem):
        arrived(ext.at[2, o], rsem.at[o, 0])
        send(ext.at[2, o, :, 0:HALF], ext.at[1, o, :, 0:HALF], ssem.at[o, 2], rsem.at[o, 2], dev(dx=1))
        arrived(ext.at[0, o], rsem.at[o, 1])
        send(
            ext.at[0, o, :, HALF:W], ext.at[1, o, :, HALF:W],
            ssem.at[o, 3], rsem.at[o, 3], dev(dx=NX - 1),
        )

    def x_third(o, ext, rsem):
        arrived(ext.at[1, o, :, 0:HALF], rsem.at[o, 2])
        arrived(ext.at[1, o, :, HALF:W], rsem.at[o, 3])

    def y_send(out, own, order, ssem, rsem):
        for g in order:
            o = (NY - g) % NY
            send(out.at[g - 1], own.at[o], ssem.at[g], rsem.at[o], dev(dy=g))

    tok_x = (xst, xrt)
    grd_x = (xsg, xrg)
    step(xg, 3, *grd_z)
    gather(xt, W + META, rt, st, lambda: x_first(0, rt, rtx, *tok_x))
    y_send(st, rt, (3, 1, 2), yst, yrt)
    step(xg, 4, *grd_z)
    for slot in range(8, 16):
        arrived(xg.at[slot], zrg.at[slot])
    gather(xg, W, rg, sg, lambda: None)
    y_send(sg, rg, (3, 2, 1), ysg, yrg)
    for load in loads:
        load.wait()
    for j in range(1, NY):
        arrived(rt.at[ORDER[j]], yrt.at[ORDER[j]])
        x_first(ORDER[j], rt, rtx, *tok_x)
        x_second(ORDER[j - 1], rtx, *tok_x)
    arrived(rg.at[BACK[0]], yrg.at[BACK[0]])
    x_first(BACK[0], rg, rgx, *grd_x)
    x_second(ORDER[3], rtx, *tok_x)

    def quarter(own, ext, o, r):
        return own[o, :, 0:W] if r == 0 else ext[r - 1, o]

    def forward(o):
        x_third(o, rtx, xrt)
        total = dot(quarter(rt, rtx, o, 0), wgu[0])
        for r in range(1, NX):
            total = total + dot(quarter(rt, rtx, o, r), wgu[r])
        gu[o] = total

    for j in range(NY):
        if j:
            if BACK[j]:
                arrived(rg.at[BACK[j]], yrg.at[BACK[j]])
            x_first(BACK[j], rg, rgx, *grd_x)
            x_second(BACK[j - 1], rgx, *grd_x)
        forward(ORDER[j])
    x_second(BACK[3], rgx, *grd_x)

    ones = jnp.ones((8, FH), BF)

    def backward(o):
        x_third(o, rgx, xrg)
        back = dot_nt(quarter(rg, rgx, o, 0), wdv[0])
        for r in range(1, NX):
            back = back + dot_nt(quarter(rg, rgx, o, r), wdv[r])
        gate = gu[o, :, 0:FH]
        up = gu[o, :, FH:2 * FH]
        sig = 1.0 / (1.0 + jnp.exp(-gate))
        act = gate * sig
        prod = act * up * back
        high = prod.astype(BF)
        low = (prod - high.astype(F32)).astype(BF)
        gx[0, o, :, 0:CH] = dot_nt(ones, high) + dot_nt(ones, low)
        for k, d in enumerate((1, 3, 2)):
            send(gx.at[0, o], gx.at[NX - d, o], gxs.at[o, k], gxr.at[o, k], dev(dx=d))
        rows = rt[o, :, W:W + META].astype(F32)
        scale = jnp.sum(
            jnp.where(iota((CH, META), 1) == me + 64, rows, 0.0), axis=1, keepdims=True
        )
        scaled = scale * back
        dgate = (scaled * up * sig * (1.0 + gate * (1.0 - sig))).astype(BF)
        dup = (scaled * act).astype(BF)
        both = jnp.concatenate([dgate, dup], axis=1)
        dd[2, o] = dot_nt(both, wgu[2]).astype(BF)
        send(dd.at[2, o, :, 0:HALF], ha.at[o], cxs.at[o, 0], cxr.at[o, 0], dev(dx=1))
        send(dd.at[2, o, :, HALF:W], hb.at[o], cxs.at[o, 1], cxr.at[o, 1], dev(dx=NX - 1))
        for r in (1, 3, 0):
            dd[r, o] = dot_nt(both, wgu[r]).astype(BF)

    def sum_second(o):
        arrived(ha.at[o], cxr.at[o, 0])
        dd[1, o, :, 0:HALF] = (dd[1, o, :, 0:HALF].astype(F32) + ha[o].astype(F32)).astype(BF)
        send(dd.at[1, o], fl.at[o], cxs.at[o, 2], cxr.at[o, 2], dev(dx=1))
        arrived(hb.at[o], cxr.at[o, 1])
        dd[3, o, :, HALF:W] = (dd[3, o, :, HALF:W].astype(F32) + hb[o].astype(F32)).astype(BF)
        send(dd.at[3, o], fr.at[o], cxs.at[o, 3], cxr.at[o, 3], dev(dx=NX - 1))

    def sum_third(o):
        g = (NY - o) % NY
        for k, d in enumerate((1, 3, 2)):
            arrived(gx.at[NX - d, o], gxr.at[o, k])
        parts = (gx[0, o] + gx[1, o]) + (gx[2, o] + gx[3, o])
        arrived(fl.at[o], cxr.at[o, 2])
        arrived(fr.at[o], cxr.at[o, 3])
        total = dd[0, o].astype(F32) + fl[o].astype(F32) + fr[o].astype(F32)
        if o == 0:
            qq[0] = total.astype(BF)
            gq[0] = parts
        else:
            vv[o] = total.astype(BF)
            gv[o] = parts
            send(vv.at[o], qq.at[g], cys.at[o], cyr.at[g], dev(dy=o))
            send(gv.at[o], gq.at[g], gys.at[o], gyr.at[g], dev(dy=o))

    for j in range(NY):
        backward(BACK[j])
        if j:
            sum_second(BACK[j - 1])
        if j > 1:
            sum_third(BACK[j - 2])
    sum_second(BACK[3])
    sum_third(BACK[2])

    for g in range(NY):
        e = (z * NY + (y + g) % NY) * NC + c
        choose = (iota((META, CH), 0) == e).astype(F32).astype(BF)
        got = dot(meta, choose)
        row, col = iota((tokens, CH), 1), iota((tokens, CH), 0)
        hit = (got == (row % CAP + 1).astype(F32)) & (row // CAP == col // ROWS)
        put[g] = jnp.where(hit, 1.0, 0.0).astype(BF)

    for n, g in enumerate((3, 2, 1)):
        arrived(qq.at[g], cyr.at[g])
        part = dot(put[g], qq[g]).reshape(SLOTS, ROWS, W)
        acc[...] = part if n == 0 else acc[...] + part
    for g in range(1, NY):
        arrived(gq.at[g], gyr.at[g])

    sum_third(BACK[3])

    def spread(lo, hi):
        own = dot(put[0, lo * ROWS:hi * ROWS, :], qq[0])
        return acc[lo:hi] + own.reshape(hi - lo, ROWS, W)

    pieces = ((3, 6), (6, 8), (0, 3))
    far = ((4, 3, 5), (6, 7), (2, 1, 0))
    for (lo, hi), ds in zip(pieces, far):
        yy[lo:hi] = spread(NZ + lo, NZ + hi).astype(BF)
        for d in ds:
            send(yy.at[d], tw.at[d], tws.at[d], twr.at[d], dev(dc=1))

    def twin_sum(d):
        arrived(tw.at[d], twr.at[d])
        bb[d] = (acc[d] + tw[d].astype(F32)).astype(BF)

    def z_send(way, h, r):
        at = slice(h * HALF, (h + 1) * HALF)
        d = NZ - r - 1 if way else r + 1
        send(
            bb.at[d, :, at], ff.at[4 * way + r, :, at], zcs.at[way, h, r], zcr.at[way, h, r],
            dev(dz=NZ - 1 if way else 1),
        )

    def z_step(way, h, r):
        at = slice(h * HALF, (h + 1) * HALF)
        d = NZ - r if way else r
        arrived(ff.at[4 * way + r, :, at], zcr.at[way, h, r])
        bb[d, :, at] = (bb[d, :, at].astype(F32) + ff[4 * way + r, :, at].astype(F32)).astype(BF)
        z_send(way, h, r - 1)

    acc[3:6] = spread(3, 6)
    twin_sum(4)
    z_send(0, 0, 3)
    z_send(1, 1, 3)
    twin_sum(3)
    z_send(0, 1, 2)
    twin_sum(5)
    z_send(1, 0, 2)
    acc[6:8] = spread(6, 8)
    acc[0:3] = spread(0, 3)

    rows8 = iota((8, 2 * META), 0)
    mine = jnp.zeros((8, 2 * META), F32)
    for g in range(NY):
        mine = mine + jnp.where(rows8 == g, gq[g], 0.0)
    gl[...] = mine
    ga[0] = mine
    for k in range(NC):
        for d in range(NZ):
            if d or k:
                slot = k * 8 + d
                back_slot = k * 8 + (NZ - d) % NZ
                send(gl, ga.at[back_slot], gzs.at[slot], gzr.at[back_slot], dev(dz=d, dc=k))

    z_step(0, 0, 3)
    z_step(1, 1, 3)
    twin_sum(2)
    z_step(0, 1, 2)
    twin_sum(6)
    z_step(1, 0, 2)
    z_step(0, 0, 2)
    z_step(1, 1, 2)
    twin_sum(1)
    z_step(0, 1, 1)
    twin_sum(7)
    z_step(1, 0, 1)
    z_step(0, 0, 1)
    z_step(1, 1, 1)

    for slot in range(1, SLOTS):
        arrived(ga.at[slot], gzr.at[slot])
    table = ga[...].reshape(SLOTS * 8, 2 * META)
    high = table.astype(BF)
    low = (table - high.astype(F32)).astype(BF)
    code = code_ref[...]
    lane8 = iota((ROWS, TOP), 1)
    result = jnp.zeros((ROWS, TOP), F32)
    for k in range(TOP):
        idk = ids_ref[:, k:k + 1]
        place = jnp.sum(jnp.where(lane == idk, code, 0.0), axis=1, keepdims=True)
        dz = ((idk >> 3) - z) & 7
        dy = ((idk >> 1) - y) & 3
        dc = (idk - c) & 1
        wanted = (dc * 8 + dz) * 8 + dy
        line = (dc * 8 + ((8 - dz) & 7)) * CAP
        onehot = (lane == wanted).astype(F32).astype(BF)
        values = dot(onehot, high) + dot(onehot, low)
        at = iota((ROWS, 2 * META), 1) - line + 1
        value = jnp.sum(jnp.where(at.astype(F32) == place, values, 0.0), axis=1, keepdims=True)
        result = result + jnp.where(lane8 == k, value, 0.0)
    gw_ref[...] = result.astype(BF)

    arrived(tw.at[0], twr.at[0])
    total = acc[0] + tw[0].astype(F32)
    for h in range(2):
        at = slice(h * HALF, (h + 1) * HALF)
        for way in range(2):
            arrived(ff.at[4 * way, :, at], zcr.at[way, h, 0])
        near = ff[0, :, at].astype(F32) + ff[4, :, at].astype(F32)
        gt_ref[:, at] = (total[:, at] + near).astype(BF)
    for copy in sends:
        copy.wait_send()


def body(tokens, grad_out, expert_ids, route_weights, gate_weights, up_weights, down_weights):
    vmem = pl.BlockSpec(memory_space=pltpu.VMEM)
    hbm = pl.BlockSpec(memory_space=pl.ANY)
    V = pltpu.VMEM
    D = pltpu.SemaphoreType.DMA
    n_tok = SLOTS * ROWS
    scratch = [
        V((SLOTS, ROWS, W + META), BF), V((SLOTS, ROWS, W), BF),
        V((NY * CH, n_tok), BF), V((NY, n_tok, CH), BF),
        V((NY - 1, CH, W + META), BF), V((NY - 1, CH, W), BF),
        V((NY, CH, W + META), BF), V((NY, CH, W), BF),
        V((NX - 1, NY, CH, W), BF), V((NX - 1, NY, CH, W), BF),
        V((NX, W, 2 * FH), BF), V((NX, FH, W), BF),
        V((NY, CH, 2 * FH), F32), V((NX, NY, CH, W), BF),
        V((NY, CH, HALF), BF), V((NY, CH, HALF), BF), V((NY, CH, W), BF), V((NY, CH, W), BF),
        V((NY, CH, W), BF), V((NY, CH, W), BF),
        V((NZ, ROWS, W), BF), V((NZ, ROWS, W), BF), V((NZ, ROWS, W), BF), V((NZ, ROWS, W), BF),
        V((NX, NY, 8, 2 * META), F32), V((NY, 8, 2 * META), F32), V((NY, 8, 2 * META), F32),
        V((8, 2 * META), F32), V((SLOTS, 8, 2 * META), F32), V((ROWS, META), F32),
        V((SLOTS, ROWS, W), F32),
        D((12,)),
        D((16,)), D((16,)), D((17,)), D((17,)),
        D((4,)), D((4,)), D((4,)), D((4,)),
        D((4, 4)), D((4, 4)), D((4, 4)), D((4, 4)),
        D((4, 4)), D((4, 4)), D((4, 3)), D((4, 3)),
        D((4,)), D((4,)), D((4,)), D((4,)),
        D((8,)), D((8,)), D((2, 2, 4)), D((2, 2, 4)), D((16,)), D((16,)),
    ]
    return pl.pallas_call(
        kernel,
        out_shape=(
            jax.ShapeDtypeStruct(tokens.shape, BF),
            jax.ShapeDtypeStruct(expert_ids.shape, BF),
        ),
        in_specs=[vmem, vmem, vmem, vmem, hbm, hbm, hbm],
        out_specs=(vmem, vmem),
        scratch_shapes=scratch,
        compiler_params=pltpu.CompilerParams(
            collective_id=0, has_side_effects=True, vmem_limit_bytes=66 * 1000 * 1000
        ),
    )(
        tokens, grad_out, expert_ids, route_weights.astype(F32),
        gate_weights, up_weights, down_weights,
    )


def solution(mesh):
    in_specs = (
        P("expert", "tensor"),
        P("expert", "tensor"),
        P("expert", None),
        P("expert", None),
        P("expert", None, "tensor"),
        P("expert", None, "tensor"),
        P("expert", "tensor", None),
    )
    out_specs = (P("expert", "tensor"), P("expert", None))
    return jax.shard_map(body, mesh=mesh, in_specs=in_specs, out_specs=out_specs, check_vma=False)
```

```python
import jax
import jax.numpy as jnp
from jax import lax
from jax.experimental import pallas as pl
from jax.experimental.pallas import tpu as pltpu
from jax.sharding import PartitionSpec as P

NZ, NY, NC, NX = 8, 4, 2, 4
TOP = 8
CAP = 9
ROWS = 64
SLOTS = NZ * NC
CH = SLOTS * CAP
W = 1024
HALF = W // 2
FH = 384
META = 128
ORDER = (0, 1, 3, 2)
BACK = (1, 2, 3, 0)
MESH = pl.DeviceIdType.MESH
F32 = jnp.float32
BF = jnp.bfloat16
NT = (((1,), (1,)), ((), ()))


def dot(a, b):
    return jnp.dot(a, b, preferred_element_type=F32)


def dot_nt(a, b):
    return lax.dot_general(a, b, NT, preferred_element_type=F32)


def iota(shape, dim):
    return lax.broadcasted_iota(jnp.int32, shape, dim)


def kernel(
    tok_ref, grd_ref, ids_ref, rw_ref, wg_ref, wu_ref, wd_ref,
    gt_ref, gw_ref,
    xt, xg, pick, put, st, sg, rt, rg, rtx, rgx, wgu, wdv, gu, dd, ha, hb, fl, fr,
    vv, qq, yy, tw, bb, ff, gx, gv, gq, gl, ga, code_ref, acc,
    w_sem, zrt, zrg, zst, zsg, yrt, yrg, yst, ysg, xrt, xrg, xst, xsg,
    cxr, cxs, gxr, gxs, cyr, cys, gyr, gys, twr, tws, zcr, zcs, gzr, gzs, opr, ops,
):
    me = lax.axis_index("expert")
    x = lax.axis_index("tensor")
    z = me // (NY * NC)
    y = (me // NC) % NY
    c = me % NC

    def dev(dz=0, dy=0, dc=0, dx=0):
        e = (((z + dz) % NZ) * NY + (y + dy) % NY) * NC + (c + dc) % NC
        return (e, (x + dx) % NX)

    def remote(src, dst, ssem, rsem, where):
        return pltpu.make_async_remote_copy(
            src_ref=src, dst_ref=dst, send_sem=ssem, recv_sem=rsem,
            device_id=where, device_id_type=MESH,
        )

    sends = []

    def send(*args):
        copy = remote(*args)
        copy.start()
        sends.append(copy)

    def arrived(dst, rsem):
        remote(dst, dst, rsem, rsem, dev(dz=1)).wait_recv()

    loads = []
    for r in range(NX):
        at = pl.multiple_of(((x + r) % NX) * W, W)
        loads.append(pltpu.make_async_copy(
            wg_ref.at[0, pl.ds(at, W), :], wgu.at[r, :, 0:FH], w_sem.at[3 * r]))
        loads.append(pltpu.make_async_copy(
            wu_ref.at[0, pl.ds(at, W), :], wgu.at[r, :, FH:2 * FH], w_sem.at[3 * r + 1]))
        loads.append(pltpu.make_async_copy(
            wd_ref.at[0, :, pl.ds(at, W)], wdv.at[r], w_sem.at[3 * r + 2]))
    for load in loads:
        load.start()

    barrier = pltpu.get_barrier_semaphore()
    partners = [dev(dz=d, dc=k) for d in range(NZ) for k in range(NC) if d or k]
    partners += [dev(dy=d) for d in range(1, NY)] + [dev(dx=d) for d in range(1, NX)]
    for partner in partners:
        pl.semaphore_signal(barrier, inc=1, device_id=partner, device_id_type=MESH)

    lane = iota((ROWS, META), 1)
    named = jnp.zeros((ROWS, META), F32)
    weight = jnp.zeros((ROWS, META), F32)
    for k in range(TOP):
        idk = ids_ref[:, k:k + 1]
        named = named + jnp.where(lane == idk, 1.0, 0.0)
        weight = weight + jnp.where(lane == idk + 64, rw_ref[:, k:k + 1], 0.0)
    below = (iota((ROWS, ROWS), 0) > iota((ROWS, ROWS), 1)).astype(F32).astype(BF)
    code = named * (dot(below, named.astype(BF)) + 1.0)
    code_ref[...] = code
    xt[0, :, 0:W] = tok_ref[...]
    xt[0, :, W:W + META] = (code + weight).astype(BF)
    xg[0, :, 0:W] = grd_ref[...]
    gx[...] = jnp.zeros_like(gx)

    pl.semaphore_wait(barrier, len(partners))

    def ring(buf, slot, rsem, ssem):
        if slot == 0:
            send(buf.at[0], buf.at[7], ssem.at[0], rsem.at[7], dev(dz=1))
            send(buf.at[0], buf.at[1], ssem.at[8], rsem.at[1], dev(dz=NZ - 1))
        elif slot > 4:
            send(buf.at[slot], buf.at[slot - 1], ssem.at[slot], rsem.at[slot - 1], dev(dz=1))
        elif slot < 3:
            send(
                buf.at[slot], buf.at[slot + 1], ssem.at[slot], rsem.at[slot + 1], dev(dz=NZ - 1)
            )
        send(buf.at[slot], buf.at[slot + 8], ssem.at[slot + 9], rsem.at[slot + 8], dev(dc=1))

    def step(buf, s, rsem, ssem):
        for slot in ((8 - s, s) if s < 4 else (4,)):
            arrived(buf.at[slot], rsem.at[slot])
            ring(buf, slot, rsem, ssem)

    tok_z = (zrt, zst)
    grd_z = (zrg, zsg)
    ring(xt, 0, *tok_z)
    send(grd_ref, xg.at[0, :, W:2 * W], ops.at[0], opr.at[0], dev(dx=2))
    for n in range(1, 4):
        step(xt, n, *tok_z)
    arrived(xg.at[0, :, W:2 * W], opr.at[0])
    ring(xg, 0, *grd_z)
    step(xt, 4, *tok_z)
    for slot in range(8, 16):
        arrived(xt.at[slot], zrt.at[slot])

    tokens = SLOTS * ROWS
    meta = xt[:, :, W:W + META].reshape(tokens, META)
    for g in range(NY):
        e = (z * NY + (y + g) % NY) * NC + c
        choose = (iota((CH, META), 1) == e).astype(F32).astype(BF)
        got = dot_nt(choose, meta)
        row, col = iota((CH, tokens), 0), iota((CH, tokens), 1)
        hit = (got == (row % CAP + 1).astype(F32)) & (row // CAP == col // ROWS)
        pick[g * CH:(g + 1) * CH, :] = jnp.where(hit, 1.0, 0.0).astype(BF)

    def gather(buf, width, own, out, rows):
        data = buf[...].reshape(tokens, width)
        own[0] = dot(pick[0:CH, :], data).astype(BF)
        rows()
        rest = dot(pick[CH:NY * CH, :], data).astype(BF)
        out[...] = rest.reshape(NY - 1, CH, width)

    def x_first(o):
        for n, lo in enumerate((0, HALF)):
            a, b = slice(lo, lo + HALF), slice(HALF - lo, W - lo)
            send(
                rt.at[o, :, a], rtx.at[2, o, :, a], xst.at[o, 2 * n], xrt.at[o, 2 * n], dev(dx=1)
            )
            send(
                rt.at[o, :, b], rtx.at[0, o, :, b],
                xst.at[o, 2 * n + 1], xrt.at[o, 2 * n + 1], dev(dx=NX - 1),
            )

    def x_second(o):
        a, b = slice(0, HALF), slice(HALF, W)
        arrived(rtx.at[2, o, :, a], xrt.at[o, 0])
        send(rtx.at[2, o, :, a], rtx.at[1, o, :, a], xst.at[o, 4], xrt.at[o, 4], dev(dx=1))
        arrived(rtx.at[0, o, :, b], xrt.at[o, 1])
        send(rtx.at[0, o, :, b], rtx.at[1, o, :, b], xst.at[o, 5], xrt.at[o, 5], dev(dx=NX - 1))

    def x_third(o):
        a, b = slice(0, HALF), slice(HALF, W)
        arrived(rtx.at[2, o, :, b], xrt.at[o, 2])
        arrived(rtx.at[0, o, :, a], xrt.at[o, 3])
        arrived(rtx.at[1, o, :, a], xrt.at[o, 4])
        arrived(rtx.at[1, o, :, b], xrt.at[o, 5])

    def x_grad(o):
        send(rg.at[o, :, 0:W], rgx.at[1, o], xsg.at[o, 0], xrg.at[o, 0], dev(dx=1))
        send(rg.at[o, :, 0:W], rgx.at[0, o], xsg.at[o, 1], xrg.at[o, 1], dev(dx=NX - 1))

    def y_send(out, own, order, ssem, rsem):
        for g in order:
            o = (NY - g) % NY
            send(out.at[g - 1], own.at[o], ssem.at[g], rsem.at[o], dev(dy=g))

    gather(xt, W + META, rt, st, lambda: x_first(0))
    y_send(st, rt, (3, 1, 2), yst, yrt)
    for j in range(1, NY):
        step(xg, j, *grd_z)
        arrived(rt.at[ORDER[j]], yrt.at[ORDER[j]])
        x_first(ORDER[j])
        x_second(ORDER[j - 1])
    step(xg, 4, *grd_z)
    for slot in range(8, 16):
        arrived(xg.at[slot], zrg.at[slot])
    gather(xg, 2 * W, rg, sg, lambda: None)
    y_send(sg, rg, (3, 2, 1), ysg, yrg)
    x_grad(0)
    x_second(ORDER[3])
    for load in loads:
        load.wait()

    def token_quarter(o, r):
        return rt[o, :, 0:W] if r == 0 else rtx[r - 1, o]

    def grad_quarter(o, r):
        return rg[o, :, r // 2 * W:(r // 2 + 1) * W] if r % 2 == 0 else rgx[r // 2, o]

    def forward(o):
        x_third(o)
        total = dot(token_quarter(o, 0), wgu[0])
        for r in range(1, NX):
            total = total + dot(token_quarter(o, r), wgu[r])
        gu[o] = total

    for j in range(NY):
        if j == NY - 1:
            arrived(rg.at[BACK[0]], yrg.at[BACK[0]])
            x_grad(BACK[0])
        forward(ORDER[j])

    ones = jnp.ones((8, FH), BF)

    def backward(o):
        arrived(rgx.at[1, o], xrg.at[o, 0])
        arrived(rgx.at[0, o], xrg.at[o, 1])
        back = dot_nt(grad_quarter(o, 0), wdv[0])
        for r in range(1, NX):
            back = back + dot_nt(grad_quarter(o, r), wdv[r])
        gate = gu[o, :, 0:FH]
        up = gu[o, :, FH:2 * FH]
        sig = 1.0 / (1.0 + jnp.exp(-gate))
        act = gate * sig
        prod = act * up * back
        high = prod.astype(BF)
        low = (prod - high.astype(F32)).astype(BF)
        gx[0, o, :, 0:CH] = dot_nt(ones, high) + dot_nt(ones, low)
        for k, d in enumerate((1, 3, 2)):
            send(gx.at[0, o], gx.at[NX - d, o], gxs.at[o, k], gxr.at[o, k], dev(dx=d))
        rows = rt[o, :, W:W + META].astype(F32)
        scale = jnp.sum(
            jnp.where(iota((CH, META), 1) == me + 64, rows, 0.0), axis=1, keepdims=True
        )
        scaled = scale * back
        dgate = (scaled * up * sig * (1.0 + gate * (1.0 - sig))).astype(BF)
        dup = (scaled * act).astype(BF)
        both = jnp.concatenate([dgate, dup], axis=1)
        dd[2, o] = dot_nt(both, wgu[2]).astype(BF)
        send(dd.at[2, o, :, 0:HALF], ha.at[o], cxs.at[o, 0], cxr.at[o, 0], dev(dx=1))
        send(dd.at[2, o, :, HALF:W], hb.at[o], cxs.at[o, 1], cxr.at[o, 1], dev(dx=NX - 1))
        for r in (1, 3, 0):
            dd[r, o] = dot_nt(both, wgu[r]).astype(BF)
            if r == 1:
                at = slice(HALF, W)
                send(dd.at[1, o, :, at], fl.at[o, :, at], cxs.at[o, 4], cxr.at[o, 4], dev(dx=1))
            if r == 3:
                at = slice(0, HALF)
                send(
                    dd.at[3, o, :, at], fr.at[o, :, at], cxs.at[o, 5], cxr.at[o, 5], dev(dx=NX - 1)
                )

    def sum_second(o):
        arrived(ha.at[o], cxr.at[o, 0])
        dd[1, o, :, 0:HALF] = (dd[1, o, :, 0:HALF].astype(F32) + ha[o].astype(F32)).astype(BF)
        send(
            dd.at[1, o, :, 0:HALF], fl.at[o, :, 0:HALF], cxs.at[o, 2], cxr.at[o, 2], dev(dx=1)
        )
        arrived(hb.at[o], cxr.at[o, 1])
        dd[3, o, :, HALF:W] = (dd[3, o, :, HALF:W].astype(F32) + hb[o].astype(F32)).astype(BF)
        send(
            dd.at[3, o, :, HALF:W], fr.at[o, :, HALF:W],
            cxs.at[o, 3], cxr.at[o, 3], dev(dx=NX - 1),
        )

    def sum_third(o):
        g = (NY - o) % NY
        for k, d in enumerate((1, 3, 2)):
            arrived(gx.at[NX - d, o], gxr.at[o, k])
        parts = (gx[0, o] + gx[1, o]) + (gx[2, o] + gx[3, o])
        arrived(fl.at[o, :, HALF:W], cxr.at[o, 4])
        arrived(fr.at[o, :, 0:HALF], cxr.at[o, 5])
        arrived(fl.at[o, :, 0:HALF], cxr.at[o, 2])
        arrived(fr.at[o, :, HALF:W], cxr.at[o, 3])
        total = dd[0, o].astype(F32) + fl[o].astype(F32) + fr[o].astype(F32)
        if o == 0:
            qq[0] = total.astype(BF)
            gq[0] = parts
        else:
            vv[o] = total.astype(BF)
            gv[o] = parts
            send(vv.at[o], qq.at[g], cys.at[o], cyr.at[g], dev(dy=o))
            send(gv.at[o], gq.at[g], gys.at[o], gyr.at[g], dev(dy=o))

    for j in range(NY):
        backward(BACK[j])
        if j < NY - 2:
            arrived(rg.at[BACK[j + 1]], yrg.at[BACK[j + 1]])
            x_grad(BACK[j + 1])
            sum_second(BACK[j])
        if j == NY - 1:
            sum_second(BACK[2])
            sum_second(BACK[3])
        if j:
            sum_third(BACK[j - 1])

    for g in range(NY):
        e = (z * NY + (y + g) % NY) * NC + c
        choose = (iota((META, CH), 0) == e).astype(F32).astype(BF)
        got = dot(meta, choose)
        row, col = iota((tokens, CH), 1), iota((tokens, CH), 0)
        hit = (got == (row % CAP + 1).astype(F32)) & (row // CAP == col // ROWS)
        put[g] = jnp.where(hit, 1.0, 0.0).astype(BF)

    for n, g in enumerate((3, 2, 1)):
        arrived(qq.at[g], cyr.at[g])
        part = dot(put[g], qq[g]).reshape(SLOTS, ROWS, W)
        acc[...] = part if n == 0 else acc[...] + part
    for g in range(1, NY):
        arrived(gq.at[g], gyr.at[g])

    sum_third(BACK[3])

    def spread(lo, hi):
        own = dot(put[0, lo * ROWS:hi * ROWS, :], qq[0])
        return acc[lo:hi] + own.reshape(hi - lo, ROWS, W)

    pieces = ((3, 6), (6, 8), (0, 3))
    far = ((4, 3, 5), (6, 7), (2, 1, 0))
    for (lo, hi), ds in zip(pieces, far):
        yy[lo:hi] = spread(NZ + lo, NZ + hi).astype(BF)
        for d in ds:
            send(yy.at[d], tw.at[d], tws.at[d], twr.at[d], dev(dc=1))

    def twin_sum(d):
        arrived(tw.at[d], twr.at[d])
        bb[d] = (acc[d] + tw[d].astype(F32)).astype(BF)

    def z_send(way, h, r):
        at = slice(h * HALF, (h + 1) * HALF)
        d = NZ - r - 1 if way else r + 1
        send(
            bb.at[d, :, at], ff.at[4 * way + r, :, at], zcs.at[way, h, r], zcr.at[way, h, r],
            dev(dz=NZ - 1 if way else 1),
        )

    def z_step(way, h, r):
        at = slice(h * HALF, (h + 1) * HALF)
        d = NZ - r if way else r
        arrived(ff.at[4 * way + r, :, at], zcr.at[way, h, r])
        bb[d, :, at] = (bb[d, :, at].astype(F32) + ff[4 * way + r, :, at].astype(F32)).astype(BF)
        z_send(way, h, r - 1)

    acc[3:6] = spread(3, 6)
    twin_sum(4)
    z_send(0, 0, 3)
    z_send(1, 1, 3)
    twin_sum(3)
    z_send(0, 1, 2)
    twin_sum(5)
    z_send(1, 0, 2)
    acc[6:8] = spread(6, 8)
    acc[0:3] = spread(0, 3)

    rows8 = iota((8, 2 * META), 0)
    mine = jnp.zeros((8, 2 * META), F32)
    for g in range(NY):
        mine = mine + jnp.where(rows8 == g, gq[g], 0.0)
    gl[...] = mine
    ga[0] = mine
    for k in range(NC):
        for d in range(NZ):
            if d or k:
                slot = k * 8 + d
                back_slot = k * 8 + (NZ - d) % NZ
                send(gl, ga.at[back_slot], gzs.at[slot], gzr.at[back_slot], dev(dz=d, dc=k))

    z_step(0, 0, 3)
    z_step(1, 1, 3)
    twin_sum(2)
    z_step(0, 1, 2)
    twin_sum(6)
    z_step(1, 0, 2)
    z_step(0, 0, 2)
    z_step(1, 1, 2)
    twin_sum(1)
    z_step(0, 1, 1)
    twin_sum(7)
    z_step(1, 0, 1)
    z_step(0, 0, 1)
    z_step(1, 1, 1)

    for slot in range(1, SLOTS):
        arrived(ga.at[slot], gzr.at[slot])
    table = ga[...].reshape(SLOTS * 8, 2 * META)
    high = table.astype(BF)
    low = (table - high.astype(F32)).astype(BF)
    code = code_ref[...]
    lane8 = iota((ROWS, TOP), 1)
    result = jnp.zeros((ROWS, TOP), F32)
    for k in range(TOP):
        idk = ids_ref[:, k:k + 1]
        place = jnp.sum(jnp.where(lane == idk, code, 0.0), axis=1, keepdims=True)
        dz = ((idk >> 3) - z) & 7
        dy = ((idk >> 1) - y) & 3
        dc = (idk - c) & 1
        wanted = (dc * 8 + dz) * 8 + dy
        line = (dc * 8 + ((8 - dz) & 7)) * CAP
        onehot = (lane == wanted).astype(F32).astype(BF)
        values = dot(onehot, high) + dot(onehot, low)
        at = iota((ROWS, 2 * META), 1) - line + 1
        value = jnp.sum(jnp.where(at.astype(F32) == place, values, 0.0), axis=1, keepdims=True)
        result = result + jnp.where(lane8 == k, value, 0.0)
    gw_ref[...] = result.astype(BF)

    arrived(tw.at[0], twr.at[0])
    total = acc[0] + tw[0].astype(F32)
    for h in range(2):
        at = slice(h * HALF, (h + 1) * HALF)
        for way in range(2):
            arrived(ff.at[4 * way, :, at], zcr.at[way, h, 0])
        near = ff[0, :, at].astype(F32) + ff[4, :, at].astype(F32)
        gt_ref[:, at] = (total[:, at] + near).astype(BF)
    for copy in sends:
        copy.wait_send()


def body(tokens, grad_out, expert_ids, route_weights, gate_weights, up_weights, down_weights):
    vmem = pl.BlockSpec(memory_space=pltpu.VMEM)
    hbm = pl.BlockSpec(memory_space=pl.ANY)
    V = pltpu.VMEM
    D = pltpu.SemaphoreType.DMA
    n_tok = SLOTS * ROWS
    scratch = [
        V((SLOTS, ROWS, W + META), BF), V((SLOTS, ROWS, 2 * W), BF),
        V((NY * CH, n_tok), BF), V((NY, n_tok, CH), BF),
        V((NY - 1, CH, W + META), BF), V((NY - 1, CH, 2 * W), BF),
        V((NY, CH, W + META), BF), V((NY, CH, 2 * W), BF),
        V((NX - 1, NY, CH, W), BF), V((2, NY, CH, W), BF),
        V((NX, W, 2 * FH), BF), V((NX, FH, W), BF),
        V((NY, CH, 2 * FH), F32), V((NX, NY, CH, W), BF),
        V((NY, CH, HALF), BF), V((NY, CH, HALF), BF), V((NY, CH, W), BF), V((NY, CH, W), BF),
        V((NY, CH, W), BF), V((NY, CH, W), BF),
        V((NZ, ROWS, W), BF), V((NZ, ROWS, W), BF), V((NZ, ROWS, W), BF), V((NZ, ROWS, W), BF),
        V((NX, NY, 8, 2 * META), F32), V((NY, 8, 2 * META), F32), V((NY, 8, 2 * META), F32),
        V((8, 2 * META), F32), V((SLOTS, 8, 2 * META), F32), V((ROWS, META), F32),
        V((SLOTS, ROWS, W), F32),
        D((12,)),
        D((16,)), D((16,)), D((17,)), D((17,)),
        D((4,)), D((4,)), D((4,)), D((4,)),
        D((4, 6)), D((4, 2)), D((4, 6)), D((4, 2)),
        D((4, 6)), D((4, 6)), D((4, 3)), D((4, 3)),
        D((4,)), D((4,)), D((4,)), D((4,)),
        D((8,)), D((8,)), D((2, 2, 4)), D((2, 2, 4)), D((16,)), D((16,)),
        D((1,)), D((1,)),
    ]
    return pl.pallas_call(
        kernel,
        out_shape=(
            jax.ShapeDtypeStruct(tokens.shape, BF),
            jax.ShapeDtypeStruct(expert_ids.shape, BF),
        ),
        in_specs=[vmem, vmem, vmem, vmem, hbm, hbm, hbm],
        out_specs=(vmem, vmem),
        scratch_shapes=scratch,
        compiler_params=pltpu.CompilerParams(
            collective_id=0, has_side_effects=True, vmem_limit_bytes=66 * 1000 * 1000
        ),
    )(
        tokens, grad_out, expert_ids, route_weights.astype(F32),
        gate_weights, up_weights, down_weights,
    )


def solution(mesh):
    in_specs = (
        P("expert", "tensor"),
        P("expert", "tensor"),
        P("expert", None),
        P("expert", None),
        P("expert", None, "tensor"),
        P("expert", None, "tensor"),
        P("expert", "tensor", None),
    )
    out_specs = (P("expert", "tensor"), P("expert", None))
    return jax.shard_map(body, mesh=mesh, in_specs=in_specs, out_specs=out_specs, check_vma=False)
```
